512 devices in a mesh: row: 16 (over y, x), col: 16 (over z), depth: 2 (over core).
Axes of the slice: x: 4, y: 4, z: 16, core: 2. Of those that a mesh axis runs over, the one named last changes fastest.
Arguments:
- features: bfloat16 [2, 16384, 1024], P('depth', ('row', 'col')), may hold values from -1.0546875 to 1.0546875
Outputs:
- drift: float32 [16384, 16384], P(('row', 'depth'), 'col')
The draws below stay inside these ranges and needn't reach their ends.
All inputs are finite; a program needn't handle non-finite values.
Results may differ from the reference program's by a relative error of at most 0.0003.
Values may be sent and summed in bfloat16 or wider, within the bound.
No kernel may reach another device: no remote copies, remote signals or barrier semaphores. Data moves between devices by JAX's collectives and lax.ppermute only.
A program may use at most 64 MiB of HBM per device.

```python
import jax
import jax.numpy as jnp
from jax import lax

FEAT = 1024
EX_DEV = 64
N = 16384
N_ROW = 16
N_COL = 16


def block_levels(key, dims, split, smallest, largest):
    factor_of, own = 1.0, jax.random.fold_in(key, 6)
    for dim, shards_of in split:
        draws = jnp.exp(jax.random.uniform(jax.random.fold_in(own, dim), (shards_of,), jnp.float32, smallest / len(split), largest / len(split)))
        factor_of = factor_of * jnp.repeat(draws, dims[dim] // shards_of).reshape([-1 if axis == dim else 1 for axis in range(len(dims))])
    return factor_of


def scatter_about(stream_key, extent, deviation, most, shards=(), held_as=jnp.bfloat16):
    array = jax.random.normal(stream_key, extent, jnp.float32) * deviation
    if len(shards) > 0:
        array = block_levels(stream_key, extent, shards, -0.22, 0.18) * array
    return jnp.clip(array, min=-most, max=most).astype(held_as)


def setup_inputs(seed: int = 0) -> dict:
    streams_of = jax.random.split(jax.random.key(seed), 2)
    features = scatter_about(streams_of[0], (2, N, FEAT), (FEAT ** -0.25), 1.0546875, ((0, 2), (1, 256)))
    return dict(features=features)


def reference(features):
    ordered = features.reshape(2, N_ROW, N_COL, EX_DEV, FEAT).transpose(0, 1, 3, 2, 4).reshape(2, N, FEAT)
    earlier_feats = ordered[0]
    later_feats = ordered[1]
    row_slabs = ordered.reshape(2, N_ROW, N // N_ROW, FEAT)

    def block_drift(blocks_in):
        later_gram = jnp.dot(blocks_in[1], later_feats.T, preferred_element_type=jnp.float32)
        earlier_gram = jnp.dot(blocks_in[0], earlier_feats.T, preferred_element_type=jnp.float32)
        return later_gram - earlier_gram

    slabs = lax.map(block_drift, (row_slabs[0], row_slabs[1]))
    return slabs.reshape(N, N)
```

```python
import jax
import jax.numpy as jnp
from jax import lax
from jax.experimental import pallas as pl
from jax.experimental.pallas import tpu as pltpu
from jax.sharding import PartitionSpec as P

STRIDE = 4


def order_rows(place_ref, group_refs, rows_ref, half):
    piece_rows = rows_ref.shape[0] // sum(ref.shape[0] for ref, _, _ in group_refs)
    start = pl.multiple_of(half * piece_rows, piece_rows)
    for ref, offset, first in group_refs:
        residue = lax.rem(place_ref[0] + offset, STRIDE)
        for g in range(ref.shape[0]):
            piece = residue + STRIDE * (first + g)
            rows_ref[pl.ds(pl.multiple_of(piece * piece_rows, piece_rows), piece_rows), :] = ref[
                g, pl.ds(start, piece_rows), :
            ]


def interleave(pieces):
    count, rows, width = pieces.shape
    return pieces.transpose(1, 0, 2).reshape(count * rows, width)


def half_product(place_ref, rows, cols, pieces):
    tile = lax.dot_general(
        rows, cols, (((1,), (1,)), ((), ())), preferred_element_type=jnp.float32
    )
    tile = tile * (2 * place_ref[1] - 1).astype(jnp.float32)
    return interleave(tile.reshape(pieces, tile.shape[0] // pieces, tile.shape[1]))


def groups_of(own_ref, before_ref, after_ref, low_ref, high_ref):
    return (
        (own_ref, 0, 0),
        (before_ref, STRIDE - 1, 0),
        (after_ref, 1, 0),
        (low_ref, 2, 0),
        (high_ref, 2, low_ref.shape[0]),
    )


def send_kernel(
    place_ref, own_ref, before_ref, after_ref, low_ref, high_ref, raw_ref,
    out_ref, cols_ref, rows_scr, turned_scr,
):
    pieces = raw_ref.shape[0]
    for j in range(pieces):
        turned_scr[j] = raw_ref[lax.rem(place_ref[0] + j, pieces)]

    @pl.when(pl.program_id(0) == 0)
    def _():
        groups = groups_of(own_ref, before_ref, after_ref, low_ref, high_ref)
        order_rows(place_ref, groups, rows_scr, 1 - place_ref[1])

    cols = interleave(turned_scr[...])
    cols_ref[...] = cols
    out_ref[...] = half_product(place_ref, rows_scr[...], cols, raw_ref.shape[0])


def keep_kernel(
    place_ref, own_ref, before_ref, after_ref, low_ref, high_ref, cols_ref, out_ref, rows_scr,
):
    @pl.when(pl.program_id(0) == 0)
    def _():
        groups = groups_of(own_ref, before_ref, after_ref, low_ref, high_ref)
        order_rows(place_ref, groups, rows_scr, place_ref[1])

    pieces = rows_scr.shape[0] * 2 // own_ref.shape[1]
    out_ref[...] = half_product(place_ref, rows_scr[...], cols_ref[...], pieces)


def partial_products(place, groups, raw):
    pieces, ex_dev, feat_width = raw.shape
    width = pieces * ex_dev
    half = width // 2
    steps = 2
    tile = width // steps
    whole = [pl.BlockSpec(g.shape, lambda n, p: (0, 0, 0)) for g in groups]
    params = pltpu.CompilerParams(
        dimension_semantics=("arbitrary",), vmem_limit_bytes=48 << 20
    )
    out_spec = pl.BlockSpec((half, tile), lambda n, p: (0, n))
    cols_spec = pl.BlockSpec((tile, feat_width), lambda n, p: (n, 0))
    rows_scr = pltpu.VMEM((half, feat_width), jnp.bfloat16)
    sent, cols = pl.pallas_call(
        send_kernel,
        out_shape=(
            jax.ShapeDtypeStruct((half, width), jnp.float32),
            jax.ShapeDtypeStruct((width, feat_width), jnp.bfloat16),
        ),
        grid_spec=pltpu.PrefetchScalarGridSpec(
            num_scalar_prefetch=1,
            grid=(steps,),
            in_specs=whole
            + [pl.BlockSpec((pieces, ex_dev // steps, feat_width), lambda n, p: (0, n, 0))],
            out_specs=(out_spec, cols_spec),
            scratch_shapes=[
                rows_scr,
                pltpu.VMEM((pieces, ex_dev // steps, feat_width), jnp.bfloat16),
            ],
        ),
        compiler_params=params,
    )(place, *groups, raw)
    kept = pl.pallas_call(
        keep_kernel,
        out_shape=jax.ShapeDtypeStruct((half, width), jnp.float32),
        grid_spec=pltpu.PrefetchScalarGridSpec(
            num_scalar_prefetch=1,
            grid=(steps,),
            in_specs=whole + [cols_spec],
            out_specs=out_spec,
            scratch_shapes=[rows_scr],
        ),
        compiler_params=params,
    )(place, *groups, cols)
    return sent, kept


def body(features):
    rows_of = lax.axis_size("row")
    cols_of = lax.axis_size("col")
    own = features[0]
    ex_dev, feat_width = own.shape
    col = lax.axis_index("col").astype(jnp.int32)
    depth = lax.axis_index("depth").astype(jnp.int32)
    members = cols_of // STRIDE

    def shifted(value, by):
        return lax.ppermute(value, "col", [(z, (z + by) % cols_of) for z in range(cols_of)])

    grid = [(r, c) for r in range(rows_of) for c in range(cols_of)]
    spread = [(r * cols_of + c, ((r + c) % rows_of) * cols_of + c) for r, c in grid]
    mirror = [(q * cols_of + c, q * cols_of + (q - c) % cols_of) for q, c in grid]
    strided = [[z + STRIDE * g for g in range(members)] for z in range(STRIDE)]

    piece = lax.ppermute(own, ("row", "col"), spread)
    held = lax.all_gather(own, "col", axis=0, tiled=False, axis_index_groups=strided)
    piece, held = lax.optimization_barrier((piece, held))
    piece = lax.ppermute(piece, ("row", "col"), mirror)

    copies = jnp.broadcast_to(piece[None], (rows_of, ex_dev, feat_width))
    raw = lax.all_to_all(copies, "row", split_axis=0, concat_axis=0, tiled=True)

    before = shifted(held, 1)
    after = shifted(held, -1)
    low = shifted(held[: members // 2], 2)
    high = shifted(held[members // 2 :], -2)

    groups = (held, before, after, low, high)
    sent, kept = partial_products(jnp.stack([col, depth]), groups, raw)
    return kept + lax.ppermute(sent, "depth", [(0, 1), (1, 0)])


def solution(mesh):
    placed = (P("depth", ("row", "col"), None),)
    return jax.shard_map(
        body, mesh=mesh, in_specs=placed, out_specs=P(("row", "depth"), "col"), check_vma=False
    )
```

```python
import jax
import jax.numpy as jnp
from jax import lax
from jax.experimental import pallas as pl
from jax.experimental.pallas import tpu as pltpu
from jax.sharding import PartitionSpec as P

STRIDE = 4
CHUNKS = 4


def interleave(pieces):
    count, rows, width = pieces.shape
    return pieces.transpose(1, 0, 2).reshape(count * rows, width)


def order_rows(place_ref, groups, rows_ref, half):
    pieces = len(groups) * groups[0].shape[0]
    piece_rows = rows_ref.shape[0] // pieces
    start = pl.multiple_of(half * piece_rows, piece_rows)
    col = place_ref[0]
    outward = 1 - 2 * place_ref[1]
    for ref, steps in zip(groups, (0, -1, 1, -2)):
        for g, far_steps in enumerate((0, -1, 1, -2)):
            hops = steps + STRIDE * far_steps
            piece = lax.rem(col + outward * hops + pieces, pieces)
            rows_ref[pl.ds(pl.multiple_of(piece * piece_rows, piece_rows), piece_rows), :] = ref[
                g, pl.ds(start, piece_rows), :
            ]


def half_product(place_ref, rows, cols, pieces):
    tile = lax.dot_general(
        rows, cols, (((1,), (1,)), ((), ())), preferred_element_type=jnp.float32
    )
    tile = tile * (2 * place_ref[1] - 1).astype(jnp.float32)
    return interleave(tile.reshape(pieces, tile.shape[0] // pieces, tile.shape[1]))


def send_kernel(
    place_ref, own_ref, before_ref, after_ref, far_ref, raw_ref,
    out_ref, cols_ref, rows_scr, turned_scr,
):
    pieces, ex_dev, _ = raw_ref.shape
    depth = place_ref[1]
    groups = (own_ref, before_ref, after_ref, far_ref)
    order_rows(place_ref, groups, rows_scr, 1 - depth)
    first = place_ref[0] + depth * (pieces // 2)
    part = ex_dev // CHUNKS
    width = part * pieces
    for n in range(CHUNKS):
        for j in range(pieces):
            turned_scr[n, j] = raw_ref[lax.rem(first + j, pieces), n * part : (n + 1) * part, :]
        cols = interleave(turned_scr[n])
        cols_ref[n * width : (n + 1) * width, :] = cols
        out_ref[:, n * width : (n + 1) * width] = half_product(
            place_ref, rows_scr[...], cols, pieces
        )


def keep_kernel(
    place_ref, own_ref, before_ref, after_ref, far_ref, cols_ref, out_ref, rows_scr,
):
    groups = (own_ref, before_ref, after_ref, far_ref)
    order_rows(place_ref, groups, rows_scr, place_ref[1])
    pieces = STRIDE * own_ref.shape[0]
    width = cols_ref.shape[0] // CHUNKS
    for n in range(CHUNKS):
        out_ref[:, n * width : (n + 1) * width] = half_product(
            place_ref, rows_scr[...], cols_ref[n * width : (n + 1) * width, :], pieces
        )


def partial_products(place, groups, raw):
    pieces, ex_dev, feat_width = raw.shape
    width = pieces * ex_dev
    half = width // 2
    in_smem = pl.BlockSpec(memory_space=pltpu.SMEM)
    whole = pl.BlockSpec(memory_space=pltpu.VMEM)
    params = pltpu.CompilerParams(vmem_limit_bytes=24 << 20)
    product = jax.ShapeDtypeStruct((half, width), jnp.float32)
    rows_scr = pltpu.VMEM((half, feat_width), jnp.bfloat16)
    sent, cols = pl.pallas_call(
        send_kernel,
        out_shape=(product, jax.ShapeDtypeStruct((width, feat_width), jnp.bfloat16)),
        in_specs=[in_smem] + [whole] * (len(groups) + 1),
        out_specs=(whole, whole),
        scratch_shapes=[
            rows_scr,
            pltpu.VMEM((CHUNKS, pieces, ex_dev // CHUNKS, feat_width), jnp.bfloat16),
        ],
        compiler_params=params,
    )(place, *groups, raw)
    kept = pl.pallas_call(
        keep_kernel,
        out_shape=product,
        in_specs=[in_smem] + [whole] * (len(groups) + 1),
        out_specs=whole,
        scratch_shapes=[rows_scr],
        compiler_params=params,
    )(place, *groups, cols)
    return sent, kept


def body(features):
    rows_of = lax.axis_size("row")
    cols_of = lax.axis_size("col")
    own = features[0]
    ex_dev, feat_width = own.shape
    col = lax.axis_index("col").astype(jnp.int32)
    depth = lax.axis_index("depth").astype(jnp.int32)

    def at(r, c, d):
        return (r % rows_of * cols_of + c % cols_of) * 2 + d

    everywhere = [(r, c, d) for r in range(rows_of) for c in range(cols_of) for d in range(2)]
    turn = rows_of // 2
    spread = [(at(r, c, d), at(r + c + turn * d, c, d)) for r, c, d in everywhere]
    mirror = [(at(q, c, d), at(q, q - turn * d - c, d)) for q, c, d in everywhere]
    axes = ("row", "col", "depth")

    def along(value, by):
        hops = [(at(r, c, d), at(r, c + by * (1 - 2 * d), d)) for r, c, d in everywhere]
        return lax.ppermute(value, axes, hops)

    piece = lax.ppermute(own, axes, spread)
    behind = along(own, STRIDE)
    ahead = along(own, -STRIDE)
    piece, behind = lax.optimization_barrier((piece, behind))
    piece = lax.ppermute(piece, axes, mirror)
    across = along(behind, STRIDE)
    piece, behind, ahead, across = lax.optimization_barrier((piece, behind, ahead, across))
    copies = jnp.broadcast_to(piece[None], (rows_of, ex_dev, feat_width))
    raw = lax.all_to_all(copies, "row", split_axis=0, concat_axis=0, tiled=True)

    held = jnp.stack([own, behind, ahead, across])
    before = along(held, 1)
    after = along(held, -1)
    far = along(before, 1)

    place = jnp.stack([col, depth])
    sent, kept = partial_products(place, (held, before, after, far), raw)
    return kept + lax.ppermute(sent, "depth", [(0, 1), (1, 0)])


def solution(mesh):
    placed = (P("depth", ("row", "col"), None),)
    return jax.shard_map(
        body, mesh=mesh, in_specs=placed, out_specs=P(("row", "depth"), "col"), check_vma=False
    )
```

```python
import jax
import jax.numpy as jnp
from jax import lax
from jax.experimental import pallas as pl
from jax.experimental.pallas import tpu as pltpu
from jax.sharding import PartitionSpec as P

STRIDE = 4
CHUNKS = 4
TURN = 5


def interleave(pieces):
    count, rows, width = pieces.shape
    return pieces.transpose(1, 0, 2).reshape(count * rows, width)


def order_rows(place_ref, groups, rows_ref, half):
    pieces = len(groups) * groups[0].shape[0]
    piece_rows = rows_ref.shape[0] // pieces
    start = pl.multiple_of(half * piece_rows, piece_rows)
    col = place_ref[0]
    outward = 1 - 2 * place_ref[1]
    for ref, steps in zip(groups, (0, -1, 1, -2)):
        for g, far_steps in enumerate((0, -1, 1, -2)):
            hops = steps + STRIDE * far_steps
            piece = lax.rem(col + outward * hops + pieces, pieces)
            rows_ref[pl.ds(pl.multiple_of(piece * piece_rows, piece_rows), piece_rows), :] = ref[
                g, pl.ds(start, piece_rows), :
            ]


def half_product(place_ref, rows, cols, pieces):
    tile = lax.dot_general(
        rows, cols, (((1,), (1,)), ((), ())), preferred_element_type=jnp.float32
    )
    tile = tile * (2 * place_ref[1] - 1).astype(jnp.float32)
    return interleave(tile.reshape(pieces, tile.shape[0] // pieces, tile.shape[1]))


def send_kernel(
    place_ref, own_ref, before_ref, after_ref, far_ref, raw_ref,
    out_ref, cols_ref, rows_scr, turned_scr,
):
    pieces, ex_dev, _ = raw_ref.shape
    depth = place_ref[1]
    groups = (own_ref, before_ref, after_ref, far_ref)
    order_rows(place_ref, groups, rows_scr, 1 - depth)
    first = place_ref[0] + depth * (pieces // 2)
    part = ex_dev // CHUNKS
    width = part * pieces
    for n in range(CHUNKS):
        for j in range(pieces):
            turned_scr[n, j] = raw_ref[lax.rem(first + (pieces - TURN) * j, pieces), n * part : (n + 1) * part, :]
        cols = interleave(turned_scr[n])
        cols_ref[n * width : (n + 1) * width, :] = cols
        out_ref[:, n * width : (n + 1) * width] = half_product(
            place_ref, rows_scr[...], cols, pieces
        )


def keep_kernel(
    place_ref, own_ref, before_ref, after_ref, far_ref, cols_ref, out_ref, rows_scr,
):
    groups = (own_ref, before_ref, after_ref, far_ref)
    order_rows(place_ref, groups, rows_scr, place_ref[1])
    pieces = STRIDE * own_ref.shape[0]
    width = cols_ref.shape[0] // CHUNKS
    for n in range(CHUNKS):
        out_ref[:, n * width : (n + 1) * width] = half_product(
            place_ref, rows_scr[...], cols_ref[n * width : (n + 1) * width, :], pieces
        )


def finish_kernel(kept_ref, came_ref, out_ref, sum_scr, sems):
    parts, rows, _ = sum_scr.shape
    stores = []
    for n in range(parts):
        band = pl.ds(n * rows, rows)
        sum_scr[n] = kept_ref[band, :] + came_ref[band, :]
        store = pltpu.make_async_copy(sum_scr.at[n], out_ref.at[band, :], sems.at[n])
        store.start()
        stores.append(store)
    for store in stores:
        store.wait()


def finished(kept, came):
    rows, width = kept.shape
    parts = 8
    whole = pl.BlockSpec(memory_space=pltpu.VMEM)
    return pl.pallas_call(
        finish_kernel,
        out_shape=jax.ShapeDtypeStruct((rows, width), jnp.float32),
        in_specs=[whole, whole],
        out_specs=pl.BlockSpec(memory_space=pltpu.HBM),
        scratch_shapes=[
            pltpu.VMEM((parts, rows // parts, width), jnp.float32),
            pltpu.SemaphoreType.DMA((parts,)),
        ],
        compiler_params=pltpu.CompilerParams(vmem_limit_bytes=16 << 20),
    )(kept, came)


def partial_products(place, groups, raw):
    pieces, ex_dev, feat_width = raw.shape
    width = pieces * ex_dev
    half = width // 2
    in_smem = pl.BlockSpec(memory_space=pltpu.SMEM)
    whole = pl.BlockSpec(memory_space=pltpu.VMEM)
    params = pltpu.CompilerParams(vmem_limit_bytes=24 << 20)
    product = jax.ShapeDtypeStruct((half, width), jnp.float32)
    rows_scr = pltpu.VMEM((half, feat_width), jnp.bfloat16)
    sent, cols = pl.pallas_call(
        send_kernel,
        out_shape=(product, jax.ShapeDtypeStruct((width, feat_width), jnp.bfloat16)),
        in_specs=[in_smem] + [whole] * (len(groups) + 1),
        out_specs=(whole, whole),
        scratch_shapes=[
            rows_scr,
            pltpu.VMEM((CHUNKS, pieces, ex_dev // CHUNKS, feat_width), jnp.bfloat16),
        ],
        compiler_params=params,
    )(place, *groups, raw)
    kept = pl.pallas_call(
        keep_kernel,
        out_shape=product,
        in_specs=[in_smem] + [whole] * (len(groups) + 1),
        out_specs=whole,
        scratch_shapes=[rows_scr],
        compiler_params=params,
    )(place, *groups, cols)
    return sent, kept


def body(features):
    rows_of = lax.axis_size("row")
    cols_of = lax.axis_size("col")
    own = features[0]
    ex_dev, feat_width = own.shape
    col = lax.axis_index("col").astype(jnp.int32)
    depth = lax.axis_index("depth").astype(jnp.int32)

    def at(r, c, d):
        return (r % rows_of * cols_of + c % cols_of) * 2 + d

    everywhere = [(r, c, d) for r in range(rows_of) for c in range(cols_of) for d in range(2)]
    turn = rows_of // 2
    spread = [(at(r, c, d), at(r - TURN * c + turn * d, c, d)) for r, c, d in everywhere]
    mirror = [(at(q, c, d), at(q, q - turn * d + TURN * c, d)) for q, c, d in everywhere]
    axes = ("row", "col", "depth")

    def along(value, by):
        hops = [(at(r, c, d), at(r, c + by * (1 - 2 * d), d)) for r, c, d in everywhere]
        return lax.ppermute(value, axes, hops)

    piece = lax.ppermute(own, axes, spread)
    behind = along(own, STRIDE)
    ahead = along(own, -STRIDE)
    piece, behind = lax.optimization_barrier((piece, behind))
    piece = lax.ppermute(piece, axes, mirror)
    across = along(behind, STRIDE)
    piece, behind, ahead, across = lax.optimization_barrier((piece, behind, ahead, across))
    copies = jnp.broadcast_to(piece[None], (rows_of, ex_dev, feat_width))
    raw = lax.all_to_all(copies, "row", split_axis=0, concat_axis=0, tiled=True)

    held = jnp.stack([own, behind, ahead, across])
    before = along(held, 1)
    after = along(held, -1)
    far = along(before, 1)

    place = jnp.stack([col, depth])
    sent, kept = partial_products(place, (held, before, after, far), raw)
    return finished(kept, lax.ppermute(sent, "depth", [(0, 1), (1, 0)]))


def solution(mesh):
    placed = (P("depth", ("row", "col"), None),)
    return jax.shard_map(
        body, mesh=mesh, in_specs=placed, out_specs=P(("row", "depth"), "col"), check_vma=False
    )
```

```python
import jax
import jax.numpy as jnp
from jax import lax
from jax.experimental import pallas as pl
from jax.experimental.pallas import tpu as pltpu
from jax.sharding import PartitionSpec as P

STRIDE = 4
CHUNKS = 4
TURN = 5


def interleave(pieces):
    count, rows, width = pieces.shape
    return pieces.transpose(1, 0, 2).reshape(count * rows, width)


def order_rows(place_ref, groups, rows_ref, half):
    pieces = len(groups) * groups[0].shape[0]
    piece_rows = rows_ref.shape[0] // pieces
    start = pl.multiple_of(half * piece_rows, piece_rows)
    col = place_ref[0]
    outward = 1 - 2 * place_ref[1]
    for ref, steps in zip(groups, (0, -1, 1, -2)):
        for g, far_steps in enumerate((0, -1, 1, -2)):
            hops = steps + STRIDE * far_steps
            piece = lax.rem(col + outward * hops + pieces, pieces)
            rows_ref[pl.ds(pl.multiple_of(piece * piece_rows, piece_rows), piece_rows), :] = ref[
                g, pl.ds(start, piece_rows), :
            ]


def half_product(place_ref, rows, cols, pieces):
    tile = lax.dot_general(
        rows, cols, (((1,), (1,)), ((), ())), preferred_element_type=jnp.float32
    )
    tile = tile * (2 * place_ref[1] - 1).astype(jnp.float32)
    return interleave(tile.reshape(pieces, tile.shape[0] // pieces, tile.shape[1]))


def send_kernel(
    place_ref, own_ref, before_ref, after_ref, far_ref, raw_ref,
    out_ref, cols_ref, rows_scr, turned_scr,
):
    pieces, ex_dev, _ = raw_ref.shape
    depth = place_ref[1]
    groups = (own_ref, before_ref, after_ref, far_ref)
    order_rows(place_ref, groups, rows_scr, 1 - depth)
    first = place_ref[0] + depth * (pieces // 2)
    part = ex_dev // CHUNKS
    width = part * pieces
    for n in range(CHUNKS):
        for j in range(pieces):
            turned_scr[n, j] = raw_ref[lax.rem(first + (pieces - TURN) * j, pieces), n * part : (n + 1) * part, :]
        cols = interleave(turned_scr[n])
        cols_ref[n * width : (n + 1) * width, :] = cols
        out_ref[:, n * width : (n + 1) * width] = half_product(
            place_ref, rows_scr[...], cols, pieces
        )


def keep_kernel(
    place_ref, own_ref, before_ref, after_ref, far_ref, cols_ref, out_ref, rows_scr,
):
    groups = (own_ref, before_ref, after_ref, far_ref)
    order_rows(place_ref, groups, rows_scr, place_ref[1])
    pieces = STRIDE * own_ref.shape[0]
    width = cols_ref.shape[0] // CHUNKS
    for n in range(CHUNKS):
        out_ref[:, n * width : (n + 1) * width] = half_product(
            place_ref, rows_scr[...], cols_ref[n * width : (n + 1) * width, :], pieces
        )


def finish_kernel(kept_ref, came_ref, out_ref, sum_scr, sems):
    parts, rows, _ = sum_scr.shape
    stores = []
    for n in range(parts):
        band = pl.ds(n * rows, rows)
        sum_scr[n] = kept_ref[band, :] + came_ref[band, :]
        store = pltpu.make_async_copy(sum_scr.at[n], out_ref.at[band, :], sems.at[n])
        store.start()
        stores.append(store)
    for store in stores:
        store.wait()


def finished(kept, came):
    rows, width = kept.shape
    parts = 8
    whole = pl.BlockSpec(memory_space=pltpu.VMEM)
    return pl.pallas_call(
        finish_kernel,
        out_shape=jax.ShapeDtypeStruct((rows, width), jnp.float32),
        in_specs=[whole, whole],
        out_specs=pl.BlockSpec(memory_space=pltpu.HBM),
        scratch_shapes=[
            pltpu.VMEM((parts, rows // parts, width), jnp.float32),
            pltpu.SemaphoreType.DMA((parts,)),
        ],
        compiler_params=pltpu.CompilerParams(vmem_limit_bytes=16 << 20),
    )(kept, came)


def partial_products(place, groups, raw):
    pieces, ex_dev, feat_width = raw.shape
    width = pieces * ex_dev
    half = width // 2
    in_smem = pl.BlockSpec(memory_space=pltpu.SMEM)
    whole = pl.BlockSpec(memory_space=pltpu.VMEM)
    params = pltpu.CompilerParams(vmem_limit_bytes=24 << 20)
    product = jax.ShapeDtypeStruct((half, width), jnp.float32)
    rows_scr = pltpu.VMEM((half, feat_width), jnp.bfloat16)
    sent, cols = pl.pallas_call(
        send_kernel,
        out_shape=(product, jax.ShapeDtypeStruct((width, feat_width), jnp.bfloat16)),
        in_specs=[in_smem] + [whole] * (len(groups) + 1),
        out_specs=(whole, whole),
        scratch_shapes=[
            rows_scr,
            pltpu.VMEM((CHUNKS, pieces, ex_dev // CHUNKS, feat_width), jnp.bfloat16),
        ],
        compiler_params=params,
    )(place, *groups, raw)
    kept = pl.pallas_call(
        keep_kernel,
        out_shape=product,
        in_specs=[in_smem] + [whole] * (len(groups) + 1),
        out_specs=whole,
        scratch_shapes=[rows_scr],
        compiler_params=params,
    )(place, *groups, cols)
    return sent, kept


def body(features):
    rows_of = lax.axis_size("row")
    cols_of = lax.axis_size("col")
    own = features[0]
    ex_dev, feat_width = own.shape
    col = lax.axis_index("col").astype(jnp.int32)
    depth = lax.axis_index("depth").astype(jnp.int32)

    def at(r, c, d):
        return (r % rows_of * cols_of + c % cols_of) * 2 + d

    everywhere = [(r, c, d) for r in range(rows_of) for c in range(cols_of) for d in range(2)]
    turn = rows_of // 2
    spread = [(at(r, c, d), at(r - TURN * c + turn * d, c, d)) for r, c, d in everywhere]
    mirror = [(at(q, c, d), at(q, q - turn * d + TURN * c, d)) for q, c, d in everywhere]
    axes = ("row", "col", "depth")

    def along(value, by):
        hops = [(at(r, c, d), at(r, c + by * (1 - 2 * d), d)) for r, c, d in everywhere]
        return lax.ppermute(value, axes, hops)

    piece = lax.ppermute(own, axes, spread)
    behind = along(own, STRIDE)
    ahead = along(own, -STRIDE)
    piece, behind = lax.optimization_barrier((piece, behind))
    piece = lax.ppermute(piece, axes, mirror)
    across = along(behind, STRIDE)
    piece, behind, ahead, across = lax.optimization_barrier((piece, behind, ahead, across))
    copies = jnp.broadcast_to(piece[None], (rows_of, ex_dev, feat_width))
    raw = lax.all_to_all(copies, "row", split_axis=0, concat_axis=0, tiled=True)

    held = jnp.stack([own, behind, ahead, across])
    before = along(held, 1)
    after = along(lax.optimization_barrier((held, before))[0], -1)
    far = along(before, 1)

    place = jnp.stack([col, depth])
    sent, kept = partial_products(place, (held, before, after, far), raw)
    return finished(kept, lax.ppermute(sent, "depth", [(0, 1), (1, 0)]))


def solution(mesh):
    placed = (P("depth", ("row", "col"), None),)
    return jax.shard_map(
        body, mesh=mesh, in_specs=placed, out_specs=P(("row", "depth"), "col"), check_vma=False
    )
```

```python
import jax
import jax.numpy as jnp
from jax import lax
from jax.experimental import pallas as pl
from jax.experimental.pallas import tpu as pltpu
from jax.sharding import PartitionSpec as P

STRIDE = 4
CHUNKS = 2
TURN = 5


def interleave(pieces):
    count, rows, width = pieces.shape
    return pieces.transpose(1, 0, 2).reshape(count * rows, width)


def order_rows(place_ref, groups, rows_ref, half):
    pieces = len(groups) * groups[0].shape[0]
    piece_rows = rows_ref.shape[0] // pieces
    start = pl.multiple_of(half * piece_rows, piece_rows)
    col = place_ref[0]
    outward = 1 - 2 * place_ref[1]
    for ref, steps in zip(groups, (0, -1, 1, -2)):
        for g, far_steps in enumerate((0, -1, 1, -2)):
            hops = steps + STRIDE * far_steps
            piece = lax.rem(col + outward * hops + pieces, pieces)
            rows_ref[pl.ds(pl.multiple_of(piece * piece_rows, piece_rows), piece_rows), :] = ref[
                g, pl.ds(start, piece_rows), :
            ]


def half_product(place_ref, rows, cols, pieces):
    tile = lax.dot_general(
        rows, cols, (((1,), (1,)), ((), ())), preferred_element_type=jnp.float32
    )
    tile = tile * (2 * place_ref[1] - 1).astype(jnp.float32)
    return interleave(tile.reshape(pieces, tile.shape[0] // pieces, tile.shape[1]))


def send_kernel(
    place_ref, own_ref, before_ref, after_ref, far_ref, raw_ref,
    out_ref, cols_ref, rows_scr, turned_scr,
):
    pieces, ex_dev, _ = raw_ref.shape
    depth = place_ref[1]
    groups = (own_ref, before_ref, after_ref, far_ref)
    order_rows(place_ref, groups, rows_scr, 1 - depth)
    first = place_ref[0] + depth * (pieces // 2)
    part = ex_dev // CHUNKS
    width = part * pieces
    for n in range(CHUNKS):
        for j in range(pieces):
            turned_scr[n, j] = raw_ref[lax.rem(first + (pieces - TURN) * j, pieces), n * part : (n + 1) * part, :]
        cols = interleave(turned_scr[n])
        cols_ref[n * width : (n + 1) * width, :] = cols
        out_ref[:, n * width : (n + 1) * width] = half_product(
            place_ref, rows_scr[...], cols, pieces
        )


def keep_kernel(
    place_ref, own_ref, before_ref, after_ref, far_ref, cols_ref, out_ref, rows_scr,
):
    groups = (own_ref, before_ref, after_ref, far_ref)
    order_rows(place_ref, groups, rows_scr, place_ref[1])
    pieces = STRIDE * own_ref.shape[0]
    width = cols_ref.shape[0] // CHUNKS
    for n in range(CHUNKS):
        out_ref[:, n * width : (n + 1) * width] = half_product(
            place_ref, rows_scr[...], cols_ref[n * width : (n + 1) * width, :], pieces
        )


def finish_kernel(kept_ref, came_ref, out_ref, sum_scr, sems):
    parts, rows, _ = sum_scr.shape
    stores = []
    for n in range(parts):
        band = pl.ds(n * rows, rows)
        sum_scr[n] = kept_ref[band, :] + came_ref[band, :]
        store = pltpu.make_async_copy(sum_scr.at[n], out_ref.at[band, :], sems.at[n])
        store.start()
        stores.append(store)
    for store in stores:
        store.wait()


def finished(kept, came):
    rows, width = kept.shape
    parts = 8
    whole = pl.BlockSpec(memory_space=pltpu.VMEM)
    return pl.pallas_call(
        finish_kernel,
        out_shape=jax.ShapeDtypeStruct((rows, width), jnp.float32),
        in_specs=[whole, whole],
        out_specs=pl.BlockSpec(memory_space=pltpu.HBM),
        scratch_shapes=[
            pltpu.VMEM((parts, rows // parts, width), jnp.float32),
            pltpu.SemaphoreType.DMA((parts,)),
        ],
        compiler_params=pltpu.CompilerParams(vmem_limit_bytes=16 << 20),
    )(kept, came)


def partial_products(place, groups, raw):
    pieces, ex_dev, feat_width = raw.shape
    width = pieces * ex_dev
    half = width // 2
    in_smem = pl.BlockSpec(memory_space=pltpu.SMEM)
    whole = pl.BlockSpec(memory_space=pltpu.VMEM)
    params = pltpu.CompilerParams(vmem_limit_bytes=24 << 20)
    product = jax.ShapeDtypeStruct((half, width), jnp.float32)
    rows_scr = pltpu.VMEM((half, feat_width), jnp.bfloat16)
    sent, cols = pl.pallas_call(
        send_kernel,
        out_shape=(product, jax.ShapeDtypeStruct((width, feat_width), jnp.bfloat16)),
        in_specs=[in_smem] + [whole] * (len(groups) + 1),
        out_specs=(whole, whole),
        scratch_shapes=[
            rows_scr,
            pltpu.VMEM((CHUNKS, pieces, ex_dev // CHUNKS, feat_width), jnp.bfloat16),
        ],
        compiler_params=params,
    )(place, *groups, raw)
    kept = pl.pallas_call(
        keep_kernel,
        out_shape=product,
        in_specs=[in_smem] + [whole] * (len(groups) + 1),
        out_specs=whole,
        scratch_shapes=[rows_scr],
        compiler_params=params,
    )(place, *groups, cols)
    return sent, kept


def body(features):
    rows_of = lax.axis_size("row")
    cols_of = lax.axis_size("col")
    own = features[0]
    ex_dev, feat_width = own.shape
    col = lax.axis_index("col").astype(jnp.int32)
    depth = lax.axis_index("depth").astype(jnp.int32)

    def at(r, c, d):
        return (r % rows_of * cols_of + c % cols_of) * 2 + d

    everywhere = [(r, c, d) for r in range(rows_of) for c in range(cols_of) for d in range(2)]
    turn = rows_of // 2
    spread = [(at(r, c, d), at(r - TURN * c + turn * d, c, d)) for r, c, d in everywhere]
    mirror = [(at(q, c, d), at(q, q - turn * d + TURN * c, d)) for q, c, d in everywhere]
    axes = ("row", "col", "depth")

    def along(value, by):
        hops = [(at(r, c, d), at(r, c + by * (1 - 2 * d), d)) for r, c, d in everywhere]
        return lax.ppermute(value, axes, hops)

    piece = lax.ppermute(own, axes, spread)
    behind = along(own, STRIDE)
    ahead = along(own, -STRIDE)
    piece, behind = lax.optimization_barrier((piece, behind))
    piece = lax.ppermute(piece, axes, mirror)
    across = along(behind, STRIDE)
    piece, behind, ahead, across = lax.optimization_barrier((piece, behind, ahead, across))
    copies = jnp.broadcast_to(piece[None], (rows_of, ex_dev, feat_width))
    raw = lax.all_to_all(copies, "row", split_axis=0, concat_axis=0, tiled=True)

    held = jnp.stack([own, behind, ahead, across])
    before = along(held, 1)
    after = along(lax.optimization_barrier((held, before))[0], -1)
    far = along(before, 1)

    place = jnp.stack([col, depth])
    sent, kept = partial_products(place, (held, before, after, far), raw)
    return finished(kept, lax.ppermute(sent, "depth", [(0, 1), (1, 0)]))


def solution(mesh):
    placed = (P("depth", ("row", "col"), None),)
    return jax.shard_map(
        body, mesh=mesh, in_specs=placed, out_specs=P(("row", "depth"), "col"), check_vma=False
    )
```
